32 devices in a mesh: dp: 8 (over y, x, core), seq: 4 (over z).
Axes of the slice: x: 2, y: 2, z: 4, core: 2. Of those that a mesh axis runs over, the one named last changes fastest.
Arguments:
- values: bfloat16 [8, 1024, 512], P('dp', 'seq'), may hold values from -6 to 6
- gates_first: bfloat16 [8, 1024, 512], P('dp', 'seq'), may hold values from -6 to 6
- gates_second: bfloat16 [8, 1024, 512], P('dp', 'seq'), may hold values from -6 to 6
- filter_early: float32 [1024, 512], P('seq'), may hold values from -4 to 4
- filter_late: float32 [1024, 512], P('seq'), may hold values from -4 to 4
- skip_early: float32 [1024], P('seq'), may hold values from 0.1 to 1.9
- skip_late: float32 [1024], P('seq'), may hold values from 0.1 to 1.9
- targets: bfloat16 [8, 512, 1024], P('dp', 'seq'), may hold values from -6 to 6
- negative_rows: int32 [8, 8, 100], P('dp', 'seq'), may hold values from 0 to 1023
- recording_ids: int32 [8], replicated, may hold values from 0 to 3
Outputs:
- values_grad: bfloat16 [8, 1024, 512], P('dp', 'seq')
- first_grad: bfloat16 [8, 1024, 512], P('dp', 'seq')
- second_grad: bfloat16 [8, 1024, 512], P('dp', 'seq')
- early_grad: float32 [1024, 512], P('seq')
- late_grad: float32 [1024, 512], P('seq')
The draws below stay inside these ranges and needn't reach their ends.
All inputs are finite; a program needn't handle non-finite values.
Results may differ from the reference program's by a relative error of at most 0.014.
Values may be sent and summed in bfloat16 or wider, within the bound.
A program may use at most 128 MiB of HBM per device.

```python
import math
import jax
import jax.numpy as jnp
from jax import lax

D = 1024
SEGMENT = 128
BLOCK = 64
NEGS = 100
FRAMES = 512
RECS = 8
N_SEQ = 4


def filter_draw(base_key):
    rate_key, noise_key = jax.random.split(base_key)
    decay_rate = jnp.exp(jax.random.uniform(rate_key, (D, 1), jnp.float32, math.log(0.5 / FRAMES), math.log(1.0 / 40.0)))
    positions = jnp.arange(FRAMES, dtype=jnp.float32)[None, :]
    envelope = jnp.exp(-decay_rate * positions)
    energy = (1.0 - jnp.exp(-2.0 * decay_rate * FRAMES)) / (1.0 - jnp.exp(-2.0 * decay_rate))
    jitter = jnp.clip(jax.random.normal(noise_key, (D, FRAMES), jnp.float32), -3.5, 3.5)
    return jitter * envelope / jnp.sqrt(energy)


def draw_filter_early(key, part):
    return filter_draw(jax.random.fold_in(key, 11))


def draw_filter_late(key, part):
    return filter_draw(jax.random.fold_in(key, 23))


def with_ends(entries, key, least, largest):
    place = [jax.random.randint(jax.random.fold_in(key, axis), (), 0, length) for axis, length in enumerate(entries.shape)]
    widest = entries.shape.index(max(entries.shape))
    neighbour = place[:widest] + [(place[widest] + 1) % entries.shape[widest]] + place[widest + 1:]
    return entries.at[tuple(place)].set(least).at[tuple(neighbour)].set(largest)


def steps_of(stream_key, dims, cuts, least, largest):
    def one(position, parts):
        steps = jax.random.uniform(jax.random.fold_in(jax.random.fold_in(stream_key, 6), position), (parts,), jnp.float32, least / len(cuts), largest / len(cuts))
        return jnp.repeat(jnp.exp(steps), dims[position] // parts).reshape((-1,) + (1,) * (len(dims) - position - 1))

    gain = one(*cuts[0])
    for cut in cuts[1:]:
        gain = gain * one(*cut)
    return gain


def centred(stream_key, dims, width, limit, cuts=(), kind=jnp.bfloat16):
    drawn = width * jax.random.normal(stream_key, dims, jnp.float32)
    if cuts:
        drawn = drawn * steps_of(stream_key, dims, cuts, -0.22, 0.18)
    return jnp.clip(drawn, -limit, limit).astype(kind)


def setup_inputs(seed: int = 0) -> dict:
    seeds = jax.random.split(jax.random.key(seed), 11)
    values = centred(seeds[0], (RECS, D, FRAMES), 1.0, 6.0, ((0, 8), (1, 4)))
    gates_first = centred(seeds[1], (RECS, D, FRAMES), 1.0, 6.0, ((0, 8), (1, 4)))
    gates_second = centred(seeds[2], (RECS, D, FRAMES), 1.0, 6.0, ((0, 8), (1, 4)))
    filter_early = draw_filter_early(jax.random.fold_in(seeds[10], 71), 0)
    filter_late = draw_filter_late(jax.random.fold_in(seeds[10], 71), 0)
    skip_early = jnp.clip(1.0 + 0.18 * jax.random.normal(seeds[5], (D,), jnp.float32), 0.1, 1.9)
    skip_late = jnp.clip(1.0 + 0.18 * jax.random.normal(seeds[6], (D,), jnp.float32), 0.1, 1.9)
    targets = centred(seeds[7], (RECS, FRAMES, D), 1.0, 6.0, ((0, 8), (1, 4)))
    negative_rows = with_ends(jax.random.randint(seeds[8], (RECS, FRAMES // BLOCK, NEGS), 0, RECS * SEGMENT), jax.random.fold_in(seeds[8], 1), 0, (RECS * SEGMENT) - 1).astype(jnp.int32)
    recording_ids = with_ends(jax.random.randint(seeds[9], (RECS,), 0, RECS // 2), jax.random.fold_in(seeds[9], 1), 0, (RECS // 2) - 1).astype(jnp.int32)
    return dict(values=values, gates_first=gates_first, gates_second=gates_second, filter_early=filter_early, filter_late=filter_late, skip_early=skip_early, skip_late=skip_late, targets=targets, negative_rows=negative_rows, recording_ids=recording_ids)


EPSILON = 1e-06
INVERSE_TEMP = 10.0
LOSS_SCALE = 256.0

def causal_conv(kernel, signal):
    length = signal.shape[-1]
    spectra = jnp.fft.rfft(signal, n=2 * length) * jnp.fft.rfft(kernel, n=2 * length)
    return jnp.fft.irfft(spectra, n=2 * length)[..., :length]

def causal_adjoint(kernel, cotangent):
    length = cotangent.shape[-1]
    spectra = jnp.fft.rfft(cotangent, n=2 * length) * jnp.conj(jnp.fft.rfft(kernel, n=2 * length))
    return jnp.fft.irfft(spectra, n=2 * length)[..., :length]

def reference(values, gates_first, gates_second, filter_early, filter_late, skip_early, skip_late, targets, negative_rows, recording_ids):

    def forward(stream):
        signal = stream[0].astype(jnp.float32)
        inner_gate = stream[1].astype(jnp.float32)
        outer_gate = stream[2].astype(jnp.float32)
        mixed_one = causal_conv(filter_early, signal) + skip_early[:, None] * signal
        hidden = inner_gate * mixed_one
        mixed_two = causal_conv(filter_late, hidden) + skip_late[:, None] * hidden
        return (mixed_one, hidden, mixed_two, outer_gate * mixed_two)
    output = lax.map(lambda stream: forward(stream)[3], (values, gates_first, gates_second))
    output_rows = jnp.transpose(output, (0, 2, 1))
    radius = jnp.sqrt(lax.optimization_barrier(jnp.sum(output_rows * output_rows, axis=-1, keepdims=True)) + EPSILON)
    unit_rows = output_rows / radius
    anchors = unit_rows.astype(jnp.bfloat16)
    target_full = targets.astype(jnp.float32)
    unit_target = (target_full / jnp.sqrt(lax.optimization_barrier(jnp.sum(target_full * target_full, axis=-1, keepdims=True)) + EPSILON)).astype(jnp.bfloat16)
    block_count = SEGMENT // BLOCK
    anchor_split = anchors.reshape(RECS, N_SEQ, SEGMENT, D).transpose(1, 0, 2, 3)
    target_split = unit_target.reshape(RECS, N_SEQ, SEGMENT, D).transpose(1, 0, 2, 3)
    index_split = negative_rows.reshape(RECS, N_SEQ, block_count, NEGS).transpose(1, 0, 2, 3)
    positions = jnp.arange(RECS * SEGMENT, dtype=jnp.int32)
    pool_ids = recording_ids[positions // SEGMENT]

    def segment_grad(inputs):
        anchor_seg, target_seg, index_seg = inputs
        pool_rows = target_seg.reshape(RECS * SEGMENT, D)

        def record_grad(members):
            anchor_rows, target_rows, index_rows, label = members
            counts = lax.optimization_barrier(jnp.sum((index_rows[:, :, None] == positions[None, None, :]).astype(jnp.float32), axis=1))
            counts = counts * (pool_ids != label).astype(jnp.float32)[None, :]
            counts = jnp.repeat(counts, BLOCK, axis=0)
            scores = jnp.dot(anchor_rows, pool_rows.T, preferred_element_type=jnp.float32) * INVERSE_TEMP
            weights = counts * jnp.exp(scores)
            target_self = target_rows.astype(jnp.float32)
            positive = jnp.exp(lax.optimization_barrier(jnp.sum(anchor_rows.astype(jnp.float32) * target_self, axis=-1)) * INVERSE_TEMP)
            totals = positive + lax.optimization_barrier(jnp.sum(weights, axis=-1))
            numerator = jnp.dot(weights.astype(jnp.bfloat16), pool_rows, preferred_element_type=jnp.float32)
            return ((positive / totals - 1.0)[:, None] * target_self + numerator / totals[:, None]) * (INVERSE_TEMP * LOSS_SCALE)
        return lax.map(record_grad, (anchor_seg, target_seg, index_seg, recording_ids))
    anchor_grad = lax.map(segment_grad, (anchor_split, target_split, index_split))
    anchor_grad = anchor_grad.transpose(1, 0, 2, 3).reshape(RECS, FRAMES, D)
    frame_grad = (anchor_grad - unit_rows * lax.optimization_barrier(jnp.sum(unit_rows * anchor_grad, axis=-1, keepdims=True))) / radius
    output_grad = jnp.transpose(frame_grad, (0, 2, 1))

    def backward(stream):
        mixed_one, hidden, mixed_two, unused = forward((stream[0], stream[1], stream[2]))
        signal = stream[0].astype(jnp.float32)
        inner_gate = stream[1].astype(jnp.float32)
        outer_gate = stream[2].astype(jnp.float32)
        cotangent = stream[3]
        second_part = (cotangent * mixed_two).astype(jnp.bfloat16)
        late_drive = cotangent * outer_gate
        hidden_grad = causal_adjoint(filter_late, late_drive) + skip_late[:, None] * late_drive
        late_update = causal_adjoint(hidden, late_drive)
        first_part = (hidden_grad * mixed_one).astype(jnp.bfloat16)
        early_drive = hidden_grad * inner_gate
        values_part = (causal_adjoint(filter_early, early_drive) + skip_early[:, None] * early_drive).astype(jnp.bfloat16)
        early_update = causal_adjoint(signal, early_drive)
        return (values_part, first_part, second_part, early_update, late_update)
    results = lax.map(backward, (values, gates_first, gates_second, output_grad))
    early_grad = lax.optimization_barrier(jnp.sum(results[3], axis=0)) / FRAMES
    late_grad = lax.optimization_barrier(jnp.sum(results[4], axis=0)) / FRAMES
    return (results[0], results[1], results[2], early_grad, late_grad)
```

```python
import functools
import math

import jax
import jax.numpy as jnp
import numpy as np
from jax import lax
from jax.experimental import pallas as pl
from jax.experimental.pallas import tpu as pltpu
from jax.sharding import PartitionSpec as P

EPSILON = 1e-06
INVERSE_TEMP = 10.0
LOSS_SCALE = 256.0
MESH = pl.DeviceIdType.MESH
F32 = jnp.float32
BF16 = jnp.bfloat16
TABLE_BYTES = 16 * 1024 * 1024
INNER_WIDTH = 128
HIGHEST = lax.Precision.HIGHEST


def shortened(value):

    def short(part):
        return part.astype(jnp.bfloat16) if part.dtype == jnp.float32 else part

    return jax.tree.map(short, value)


def twiddle(row_count, column_count, length, direction):
    product = (
        jnp.arange(row_count, dtype=jnp.int32)[:, None]
        * jnp.arange(column_count, dtype=jnp.int32)[None, :]
        % length
    )
    angles = direction * 2.0 * math.pi / length * product.astype(jnp.float32)
    return (jnp.cos(angles), jnp.sin(angles))


def complex_table(cosines, sines, with_imaginary):
    upper = jnp.concatenate([cosines, sines], axis=1)
    if not with_imaginary:
        return upper
    lower = jnp.concatenate([-sines, cosines], axis=1)
    return jnp.concatenate([upper, lower], axis=0)


def transform(real_part, imaginary, direction, length):
    used = real_part.shape[-1]
    with_imaginary = imaginary is not None
    outer_size = length // INNER_WIDTH
    used_rows = used // INNER_WIDTH
    lead = real_part.shape[:-1]
    folded_real = real_part.reshape(lead + (used_rows, INNER_WIDTH))
    cosines, sines = twiddle(used_rows, outer_size, outer_size, direction)
    table = complex_table(cosines, sines, with_imaginary)
    if with_imaginary:
        stacked = jnp.concatenate(
            [folded_real, imaginary.reshape(lead + (used_rows, INNER_WIDTH))], axis=-2
        )
    else:
        stacked = folded_real
    section = jnp.einsum("...ab,ak->...kb", stacked, table, precision=HIGHEST)
    section_real = section[..., :outer_size, :]
    section_imaginary = section[..., outer_size:, :]
    turn_cosine, turn_sine = twiddle(outer_size, INNER_WIDTH, length, direction)
    turned_real = section_real * turn_cosine - section_imaginary * turn_sine
    turned_imaginary = section_real * turn_sine + section_imaginary * turn_cosine
    inner_cosine, inner_sine = twiddle(INNER_WIDTH, INNER_WIDTH, INNER_WIDTH, direction)
    inner_table = complex_table(inner_cosine, inner_sine, True)
    second = jnp.einsum(
        "...ab,bk->...ak",
        jnp.concatenate([turned_real, turned_imaginary], axis=-1),
        inner_table,
        precision=HIGHEST,
    )
    final_real = jnp.swapaxes(second[..., :INNER_WIDTH], -1, -2).reshape(lead + (length,))
    final_imaginary = jnp.swapaxes(second[..., INNER_WIDTH:], -1, -2).reshape(lead + (length,))
    return (final_real, final_imaginary)


def spectrum(signal):
    return transform(signal, None, -1.0, 2 * signal.shape[-1])


def split_pair(first_signal, second_signal):
    spec_real, spec_imaginary = transform(
        first_signal, second_signal, -1.0, 2 * first_signal.shape[-1]
    )
    mirror_real = jnp.roll(jnp.flip(spec_real, -1), 1, -1)
    mirror_imaginary = jnp.roll(jnp.flip(spec_imaginary, -1), 1, -1)
    first_spec = ((spec_real + mirror_real) * 0.5, (spec_imaginary - mirror_imaginary) * 0.5)
    second_spec = ((spec_imaginary + mirror_imaginary) * 0.5, (mirror_real - spec_real) * 0.5)
    return (first_spec, second_spec)


def multiply(left_side, right_side):
    return (
        left_side[0] * right_side[0] - left_side[1] * right_side[1],
        left_side[0] * right_side[1] + left_side[1] * right_side[0],
    )


def conjugate(spec):
    return (spec[0], -spec[1])


def combine(left_side, right_side):
    return (left_side[0] - right_side[1], left_side[1] + right_side[0])


def inverse(spec, frames):
    length = spec[0].shape[-1]
    out_real, out_imaginary = transform(spec[0], spec[1], 1.0, length)
    factor = 1.0 / length
    return (out_real[..., :frames] * factor, out_imaginary[..., :frames] * factor)


def local_large(
    values,
    gates_first,
    gates_second,
    filter_early,
    filter_late,
    skip_early,
    skip_late,
    targets,
    negative_rows,
    recording_ids,
):
    signal = values[0].astype(jnp.float32)
    inner_gate = gates_first[0].astype(jnp.float32)
    outer_gate = gates_second[0].astype(jnp.float32)
    frames = signal.shape[-1]
    early_skip = skip_early[:, None]
    late_skip = skip_late[:, None]
    target_full = targets[0].astype(jnp.float32)
    unit_target = (
        target_full / jnp.sqrt(jnp.sum(target_full * target_full, axis=-1, keepdims=True) + EPSILON)
    ).astype(jnp.bfloat16)
    signal_spec, early_spec = split_pair(signal, filter_early)
    mixed_one = inverse(multiply(signal_spec, early_spec), frames)[0] + early_skip * signal
    hidden = inner_gate * mixed_one
    hidden_spec, late_spec = split_pair(hidden, filter_late)
    mixed_two = inverse(multiply(hidden_spec, late_spec), frames)[0] + late_skip * hidden
    output = outer_gate * mixed_two
    arrived = lax.all_to_all(
        output[None].astype(jnp.bfloat16), "seq", split_axis=2, concat_axis=1, tiled=True
    ).astype(jnp.float32)
    output_rows = jnp.transpose(arrived[0])
    radius = jnp.sqrt(jnp.sum(output_rows * output_rows, axis=-1, keepdims=True) + EPSILON)
    unit_rows = output_rows / radius
    anchors = unit_rows.astype(jnp.bfloat16)
    own_record = lax.axis_index("dp")
    record_count = recording_ids.shape[0]
    record_range = jnp.arange(record_count, dtype=jnp.int32)
    self_label = jnp.sum(jnp.where(record_range == own_record, recording_ids, 0))
    segment = anchors.shape[0]
    block_rows = negative_rows[0]
    block_count = block_rows.shape[0]
    block_size = segment // block_count
    column_ids = jnp.arange(segment, dtype=jnp.int32)
    initial = (
        jnp.zeros((segment,), jnp.float32),
        jnp.zeros((segment, anchors.shape[1]), jnp.float32),
    )
    shard_rows = lax.all_gather(unit_target[None], "dp", axis=0, tiled=True)

    def one_record(partial_value, member):
        pool_rows, record = member
        label = jnp.sum(jnp.where(record_range == record, recording_ids, 0))
        allowed = (label != self_label).astype(jnp.float32)
        matches = (block_rows[:, :, None] == (record * segment + column_ids)[None, None, :]).astype(
            jnp.float32
        )
        counts = jnp.sum(matches, axis=1) * allowed
        counts = jnp.broadcast_to(counts[:, None, :], (block_count, block_size, segment)).reshape(
            segment, segment
        )
        scores = (
            lax.dot_general(
                anchors, pool_rows, (((1,), (1,)), ((), ())), preferred_element_type=jnp.float32
            )
            * INVERSE_TEMP
        )
        weights = counts * jnp.exp(scores)
        numerator = jnp.dot(
            weights.astype(jnp.bfloat16), pool_rows, preferred_element_type=jnp.float32
        )
        return ((partial_value[0] + jnp.sum(weights, axis=-1), partial_value[1] + numerator), None)

    records = jnp.arange(shard_rows.shape[0], dtype=jnp.int32)
    summed = lax.scan(one_record, initial, (shard_rows, records))[0]
    unit_self = unit_target.astype(jnp.float32)
    positive = jnp.exp(jnp.sum(anchors.astype(jnp.float32) * unit_self, axis=-1) * INVERSE_TEMP)
    totals = positive + summed[0]
    anchor_grad = ((positive / totals - 1.0)[:, None] * unit_self + summed[1] / totals[:, None]) * (
        INVERSE_TEMP * LOSS_SCALE
    )
    frame_grad = (
        anchor_grad - unit_rows * jnp.sum(unit_rows * anchor_grad, axis=-1, keepdims=True)
    ) / radius
    arrived_back = lax.all_to_all(
        shortened(jnp.transpose(frame_grad)[None]), "seq", split_axis=1, concat_axis=2, tiled=True
    )
    cotangent = arrived_back[0]
    second_grad = (cotangent * mixed_two).astype(jnp.bfloat16)
    late_drive = cotangent * outer_gate
    back_late = spectrum(late_drive)
    late_pair = combine(
        multiply(back_late, conjugate(late_spec)), multiply(back_late, conjugate(hidden_spec))
    )
    hidden_back, late_update = inverse(late_pair, frames)
    hidden_grad = hidden_back + late_skip * late_drive
    first_grad = (hidden_grad * mixed_one).astype(jnp.bfloat16)
    early_drive = hidden_grad * inner_gate
    back_early = spectrum(early_drive)
    early_pair = combine(
        multiply(back_early, conjugate(early_spec)), multiply(back_early, conjugate(signal_spec))
    )
    signal_back, early_update = inverse(early_pair, frames)
    values_grad = (signal_back + early_skip * early_drive).astype(jnp.bfloat16)
    filter_sums = (
        lax.psum(early_update.astype(jnp.bfloat16), "dp").astype(jnp.float32),
        lax.psum(late_update.astype(jnp.bfloat16), "dp").astype(jnp.float32),
    )
    return (
        values_grad[None],
        first_grad[None],
        second_grad[None],
        filter_sums[0] / frames,
        filter_sums[1] / frames,
    )


def tables(frames):
    odd = 2 * np.arange(frames, dtype=np.int64) + 1
    period = 8 * frames
    circle = 2.0 * np.pi / period * np.arange(period)
    product = odd[:, None] * odd[None, :] % period
    highs, lows = [], []
    for wave in (np.cos(circle), np.sin(circle)):
        wave = wave.astype(np.float32)
        high = wave.astype(BF16)
        low = (wave - high.astype(np.float32)).astype(BF16)
        highs.append(high[product])
        lows.append(low[product])
    half = np.pi * odd / (4.0 * frames)
    turn = np.stack([np.cos(half), np.sin(half)]) / frames
    return np.stack(highs), np.stack(lows), turn.astype(np.float32)


def halves(value):
    high = value.astype(BF16)
    return high, (value - high.astype(F32)).astype(BF16)


def product(parts, table_high, table_low):
    high, low = parts
    total = jnp.dot(high, table_high, preferred_element_type=F32)
    total += jnp.dot(high, table_low, preferred_element_type=F32)
    if low is not None:
        total += jnp.dot(low, table_high, preferred_element_type=F32)
    return total


def kernel(
    sizes,
    values_ref, first_ref, second_ref, early_ref, late_ref, early_skip_ref, late_skip_ref,
    targets_ref, rows_ref, ids_ref, high_ref, low_ref, turn_ref,
    values_out, first_out, second_out, early_out, late_out,
    pool, out_send, out_recv, back_send, back_recv, reduce_send, reduce_recv,
    mixed_one, mixed_two, early_spec, late_spec, signal_spec, hidden_spec,
    pool_send_sem, pool_recv_sem, pass_send_sem, pass_recv_sem,
    out_send_sem, out_recv_sem, back_send_sem, back_recv_sem,
    reduce_send_sem, reduce_recv_sem, share_send_sem, share_recv_sem,
):
    records, stages = sizes
    chips = records // 2
    me = lax.axis_index("dp")
    here = lax.axis_index("seq")
    chip, core = me // 2, me % 2
    partner = chip * 2 + (1 - core)
    channels, frames = mixed_one.shape
    segment = pool.shape[1]
    depth = pool.shape[2]

    barrier = pltpu.get_barrier_semaphore()
    for k in range(1, records):
        pl.semaphore_signal(
            barrier, inc=1, device_id=(lax.rem(me + k, records), here), device_id_type=MESH
        )
    for k in range(1, stages):
        pl.semaphore_signal(
            barrier, inc=1, device_id=(me, lax.rem(here + k, stages)), device_id_type=MESH
        )

    def remote(source, target, send, recv, device):
        return pltpu.make_async_remote_copy(
            src_ref=source, dst_ref=target, send_sem=send, recv_sem=recv,
            device_id=device, device_id_type=MESH,
        )

    full = targets_ref[0].astype(F32)
    norm = jnp.sqrt(jnp.sum(full * full, axis=-1, keepdims=True) + EPSILON)
    pool[me] = (full / norm).astype(BF16)
    pl.semaphore_wait(barrier, records + stages - 2)

    def pool_copy(k):
        peer = lax.rem(chip + k, chips) * 2 + core
        return remote(pool.at[me], pool.at[me], pool_send_sem.at[k], pool_recv_sem.at[k], (peer, here))

    def pool_arrival(k):
        slot = lax.rem(chip + chips - k, chips) * 2 + core
        return slot, remote(
            pool.at[slot], pool.at[slot], pool_send_sem.at[k], pool_recv_sem.at[k], (slot, here)
        )

    def pass_copy(k):
        slot = lax.rem(chip + chips - k, chips) * 2 + core
        return remote(
            pool.at[slot], pool.at[slot], pass_send_sem.at[k], pass_recv_sem.at[k], (partner, here)
        )

    def pass_arrival(k):
        slot = lax.rem(chip + chips - k, chips) * 2 + (1 - core)
        return remote(
            pool.at[slot], pool.at[slot], pass_send_sem.at[k], pass_recv_sem.at[k], (partner, here)
        )

    for k in range(1, chips):
        pool_copy(k).start()
    pass_copy(0).start()

    def forward(parts):
        return tuple(product(parts, high_ref[i], low_ref[i]) for i in (0, 1))

    def inverse(cosine, sine):
        return product(halves(cosine), high_ref[0], low_ref[0]) + product(
            halves(sine), high_ref[1], low_ref[1]
        )

    def unshifted(spec):
        cosine, sine = spec
        turn_cosine = turn_ref[0:1, :]
        turn_sine = turn_ref[1:2, :]
        return (
            cosine * turn_cosine + sine * turn_sine,
            sine * turn_cosine - cosine * turn_sine,
        )

    def keep(ref, spec):
        ref[0] = spec[0]
        ref[1] = spec[1]

    def convolved(spec, ref):
        cosine, sine = spec
        return inverse(cosine * ref[0] - sine * ref[1], cosine * ref[1] + sine * ref[0])

    def correlated(spec, ref):
        cosine, sine = spec
        return inverse(cosine * ref[0] + sine * ref[1], sine * ref[0] - cosine * ref[1])

    keep(early_spec, unshifted(forward(halves(early_ref[...]))))
    keep(late_spec, unshifted(forward(halves(late_ref[...]))))
    spec = forward((values_ref[0], None))
    mixed_one[...] = convolved(spec, early_spec) + early_skip_ref[...] * values_ref[0].astype(F32)
    keep(signal_spec, unshifted(spec))
    hidden = first_ref[0].astype(F32) * mixed_one[...]
    spec = forward(halves(hidden))
    mixed_two[...] = convolved(spec, late_spec) + late_skip_ref[...] * hidden
    keep(hidden_spec, unshifted(spec))

    output = second_ref[0].astype(F32) * mixed_two[...]
    for s in range(stages):
        out_send[s] = output[:, s * segment : (s + 1) * segment].astype(BF16)

    def exchange(k, send, recv, send_sem, recv_sem):
        peer = lax.rem(here + k, stages)
        return remote(send.at[peer], recv.at[here], send_sem.at[k], recv_sem.at[k], (me, peer))

    def exchange_arrival(k, send, recv, send_sem, recv_sem):
        peer = lax.rem(here + stages - k, stages)
        return remote(send.at[peer], recv.at[peer], send_sem.at[k], recv_sem.at[k], (me, peer))

    out_group = (out_send, out_recv, out_send_sem, out_recv_sem)
    back_group = (back_send, back_recv, back_send_sem, back_recv_sem)
    for k in range(1, stages):
        exchange(k, *out_group).start()
    out_recv[here] = out_send[here]

    for k in range(1, chips):
        pool_arrival(k)[1].wait_recv()
        pass_copy(k).start()

    blocks = rows_ref.shape[0]
    draws = rows_ref.shape[1]
    block_size = segment // blocks
    frame_block = lax.broadcasted_iota(jnp.int32, (draws, segment), 1) // block_size
    counts = jnp.zeros((records * segment, segment), F32)
    position = lax.broadcasted_iota(jnp.int32, (records * segment, draws), 0)
    for b in range(blocks):
        matches = jnp.where(position == rows_ref[b : b + 1, :], 1.0, 0.0).astype(BF16)
        chosen = jnp.where(frame_block == b, 1.0, 0.0).astype(BF16)
        counts += jnp.dot(matches, chosen, preferred_element_type=F32)

    self_units = pool[me].astype(F32).T

    for k in range(1, stages):
        exchange_arrival(k, *out_group).wait_recv()
    rows = jnp.concatenate([out_recv[s] for s in range(stages)], axis=0).astype(F32)
    radius = jnp.sqrt(jnp.sum(rows * rows, axis=0, keepdims=True) + EPSILON)
    unit_rows = rows / radius
    anchors = unit_rows.astype(BF16)
    positive = jnp.exp(jnp.sum(anchors.astype(F32) * self_units, axis=0, keepdims=True) * INVERSE_TEMP)

    for k in range(chips):
        pass_arrival(k).wait_recv()

    totals = positive
    numerator = jnp.zeros((segment, depth), F32)
    for q in range(records):
        units = pool[q]
        allowed = jnp.where(ids_ref[q] != ids_ref[me], 1.0, 0.0).astype(F32)
        scores = jnp.dot(units, anchors, preferred_element_type=F32) * INVERSE_TEMP
        weights = counts[q * segment : (q + 1) * segment, :] * allowed * jnp.exp(scores)
        totals += jnp.sum(weights, axis=0, keepdims=True)
        numerator += jnp.dot(weights.T.astype(BF16), units, preferred_element_type=F32)
    anchor_grad = ((positive / totals - 1.0) * self_units + numerator.T / totals) * (
        INVERSE_TEMP * LOSS_SCALE
    )
    frame_grad = (
        anchor_grad - unit_rows * jnp.sum(unit_rows * anchor_grad, axis=0, keepdims=True)
    ) / radius
    for s in range(stages):
        back_send[s] = frame_grad[s * channels : (s + 1) * channels, :].astype(BF16)
    for k in range(1, stages):
        exchange(k, *back_group).start()
    back_recv[here] = back_send[here]
    for k in range(1, stages):
        exchange_arrival(k, *back_group).wait_recv()

    cotangent = jnp.concatenate([back_recv[s] for s in range(stages)], axis=1).astype(F32)
    second_out[0] = (cotangent * mixed_two[...]).astype(BF16)
    late_drive = cotangent * second_ref[0].astype(F32)
    spec = forward(halves(late_drive))

    shard = channels // records

    def spread(which, update):
        for r in range(records):
            reduce_send[which, r] = update[r * shard : (r + 1) * shard, :].astype(BF16)
        for k in range(1, records):
            peer = lax.rem(me + k, records)
            remote(
                reduce_send.at[which, peer], reduce_recv.at[which, me],
                reduce_send_sem.at[which, k], reduce_recv_sem.at[which, k], (peer, here),
            ).start()

    def share(which, target):
        for k in range(1, records):
            peer = lax.rem(me + records - k, records)
            remote(
                reduce_send.at[which, peer], reduce_recv.at[which, peer],
                reduce_send_sem.at[which, k], reduce_recv_sem.at[which, k], (peer, here),
            ).wait_recv()
        total = reduce_send[which, me].astype(F32)
        for k in range(1, records):
            total += reduce_recv[which, lax.rem(me + records - k, records)].astype(F32)
        target[me] = total.astype(BF16)
        for k in range(1, records):
            peer = lax.rem(me + k, records)
            remote(
                target.at[me], target.at[me],
                share_send_sem.at[which, k], share_recv_sem.at[which, k], (peer, here),
            ).start()

    spread(1, correlated(spec, hidden_spec))
    hidden_grad = correlated(spec, late_spec) + late_skip_ref[...] * late_drive
    first_out[0] = (hidden_grad * mixed_one[...]).astype(BF16)
    early_drive = hidden_grad * first_ref[0].astype(F32)
    spec = forward(halves(early_drive))
    spread(0, correlated(spec, signal_spec))
    share(1, late_out)
    values_out[0] = (correlated(spec, early_spec) + early_skip_ref[...] * early_drive).astype(BF16)
    share(0, early_out)

    for k in range(1, chips):
        pool_copy(k).wait_send()
    for k in range(chips):
        pass_copy(k).wait_send()
    for k in range(1, stages):
        exchange(k, *out_group).wait_send()
        exchange(k, *back_group).wait_send()
    for which, target in ((1, late_out), (0, early_out)):
        for k in range(1, records):
            peer = lax.rem(me + k, records)
            remote(
                reduce_send.at[which, peer], reduce_recv.at[which, me],
                reduce_send_sem.at[which, k], reduce_recv_sem.at[which, k], (peer, here),
            ).wait_send()
            source = lax.rem(me + records - k, records)
            shared = remote(
                target.at[source], target.at[source],
                share_send_sem.at[which, k], share_recv_sem.at[which, k], (source, here),
            )
            shared.wait_recv()
            shared.wait_send()


def local(
    records, stages,
    values, gates_first, gates_second, filter_early, filter_late, skip_early, skip_late,
    targets, negative_rows, recording_ids,
):
    _, channels, frames = values.shape
    _, segment, depth = targets.shape
    if 8 * frames * frames > TABLE_BYTES:
        return local_large(
            values, gates_first, gates_second, filter_early, filter_late, skip_early, skip_late,
            targets, negative_rows, recording_ids,
        )
    high, low, turn = tables(frames)
    draws = negative_rows.shape[2]
    padded = -(-draws // 128) * 128
    block_rows = jnp.pad(negative_rows[0], ((0, 0), (0, padded - draws)), constant_values=-1)
    shard = channels // records
    vmem = pl.BlockSpec(memory_space=pltpu.VMEM)
    stream = jax.ShapeDtypeStruct(values.shape, BF16)
    update = jax.ShapeDtypeStruct((records, shard, frames), BF16)
    exchange = pltpu.VMEM((stages, channels, segment), BF16)
    reduce = pltpu.VMEM((2, records, shard, frames), BF16)
    plane = pltpu.VMEM((channels, frames), F32)
    spec = pltpu.VMEM((2, channels, frames), F32)
    semaphores = pltpu.SemaphoreType.DMA
    chips = records // 2
    results = pl.pallas_call(
        functools.partial(kernel, (records, stages)),
        out_shape=(stream, stream, stream, update, update),
        in_specs=[vmem] * 9 + [pl.BlockSpec(memory_space=pltpu.SMEM)] + [vmem] * 3,
        out_specs=(vmem,) * 5,
        scratch_shapes=[
            pltpu.VMEM((records, segment, depth), BF16),
            exchange, exchange, exchange, exchange, reduce, reduce,
            plane, plane, spec, spec, spec, spec,
            semaphores((chips,)), semaphores((chips,)), semaphores((chips,)), semaphores((chips,)),
            semaphores((stages,)), semaphores((stages,)), semaphores((stages,)), semaphores((stages,)),
            semaphores((2, records)), semaphores((2, records)),
            semaphores((2, records)), semaphores((2, records)),
        ],
        compiler_params=pltpu.CompilerParams(
            collective_id=0, has_side_effects=True, vmem_limit_bytes=63 * 1024 * 1024
        ),
    )(
        values, gates_first, gates_second, filter_early, filter_late,
        skip_early[:, None], skip_late[:, None], targets, block_rows, recording_ids,
        jnp.asarray(high), jnp.asarray(low), jnp.asarray(turn),
    )
    early = results[3].reshape(channels, frames).astype(F32) / frames
    late = results[4].reshape(channels, frames).astype(F32) / frames
    return results[0], results[1], results[2], early, late


def solution(mesh):
    placed = (
        P("dp", "seq", None),
        P("dp", "seq", None),
        P("dp", "seq", None),
        P("seq", None),
        P("seq", None),
        P("seq"),
        P("seq"),
        P("dp", "seq", None),
        P("dp", "seq", None),
        P(),
    )
    return jax.shard_map(
        functools.partial(local, mesh.shape["dp"], mesh.shape["seq"]),
        mesh=mesh,
        in_specs=placed,
        out_specs=(
            P("dp", "seq", None),
            P("dp", "seq", None),
            P("dp", "seq", None),
            P("seq", None),
            P("seq", None),
        ),
        check_vma=False,
    )
```

```python
import functools
import math

import jax
import jax.numpy as jnp
import numpy as np
from jax import lax
from jax.experimental import pallas as pl
from jax.experimental.pallas import tpu as pltpu
from jax.sharding import PartitionSpec as P

EPSILON = 1e-06
INVERSE_TEMP = 10.0
LOSS_SCALE = 256.0
MESH = pl.DeviceIdType.MESH
F32 = jnp.float32
BF16 = jnp.bfloat16
TABLE_BYTES = 16 * 1024 * 1024
INNER_WIDTH = 128
HIGHEST = lax.Precision.HIGHEST


def shortened(value):

    def short(part):
        return part.astype(jnp.bfloat16) if part.dtype == jnp.float32 else part

    return jax.tree.map(short, value)


def twiddle(row_count, column_count, length, direction):
    product = (
        jnp.arange(row_count, dtype=jnp.int32)[:, None]
        * jnp.arange(column_count, dtype=jnp.int32)[None, :]
        % length
    )
    angles = direction * 2.0 * math.pi / length * product.astype(jnp.float32)
    return (jnp.cos(angles), jnp.sin(angles))


def complex_table(cosines, sines, with_imaginary):
    upper = jnp.concatenate([cosines, sines], axis=1)
    if not with_imaginary:
        return upper
    lower = jnp.concatenate([-sines, cosines], axis=1)
    return jnp.concatenate([upper, lower], axis=0)


def transform(real_part, imaginary, direction, length):
    used = real_part.shape[-1]
    with_imaginary = imaginary is not None
    outer_size = length // INNER_WIDTH
    used_rows = used // INNER_WIDTH
    lead = real_part.shape[:-1]
    folded_real = real_part.reshape(lead + (used_rows, INNER_WIDTH))
    cosines, sines = twiddle(used_rows, outer_size, outer_size, direction)
    table = complex_table(cosines, sines, with_imaginary)
    if with_imaginary:
        stacked = jnp.concatenate(
            [folded_real, imaginary.reshape(lead + (used_rows, INNER_WIDTH))], axis=-2
        )
    else:
        stacked = folded_real
    section = jnp.einsum("...ab,ak->...kb", stacked, table, precision=HIGHEST)
    section_real = section[..., :outer_size, :]
    section_imaginary = section[..., outer_size:, :]
    turn_cosine, turn_sine = twiddle(outer_size, INNER_WIDTH, length, direction)
    turned_real = section_real * turn_cosine - section_imaginary * turn_sine
    turned_imaginary = section_real * turn_sine + section_imaginary * turn_cosine
    inner_cosine, inner_sine = twiddle(INNER_WIDTH, INNER_WIDTH, INNER_WIDTH, direction)
    inner_table = complex_table(inner_cosine, inner_sine, True)
    second = jnp.einsum(
        "...ab,bk->...ak",
        jnp.concatenate([turned_real, turned_imaginary], axis=-1),
        inner_table,
        precision=HIGHEST,
    )
    final_real = jnp.swapaxes(second[..., :INNER_WIDTH], -1, -2).reshape(lead + (length,))
    final_imaginary = jnp.swapaxes(second[..., INNER_WIDTH:], -1, -2).reshape(lead + (length,))
    return (final_real, final_imaginary)


def spectrum(signal):
    return transform(signal, None, -1.0, 2 * signal.shape[-1])


def split_pair(first_signal, second_signal):
    spec_real, spec_imaginary = transform(
        first_signal, second_signal, -1.0, 2 * first_signal.shape[-1]
    )
    mirror_real = jnp.roll(jnp.flip(spec_real, -1), 1, -1)
    mirror_imaginary = jnp.roll(jnp.flip(spec_imaginary, -1), 1, -1)
    first_spec = ((spec_real + mirror_real) * 0.5, (spec_imaginary - mirror_imaginary) * 0.5)
    second_spec = ((spec_imaginary + mirror_imaginary) * 0.5, (mirror_real - spec_real) * 0.5)
    return (first_spec, second_spec)


def multiply(left_side, right_side):
    return (
        left_side[0] * right_side[0] - left_side[1] * right_side[1],
        left_side[0] * right_side[1] + left_side[1] * right_side[0],
    )


def conjugate(spec):
    return (spec[0], -spec[1])


def combine(left_side, right_side):
    return (left_side[0] - right_side[1], left_side[1] + right_side[0])


def inverse(spec, frames):
    length = spec[0].shape[-1]
    out_real, out_imaginary = transform(spec[0], spec[1], 1.0, length)
    factor = 1.0 / length
    return (out_real[..., :frames] * factor, out_imaginary[..., :frames] * factor)


def local_large(
    values,
    gates_first,
    gates_second,
    filter_early,
    filter_late,
    skip_early,
    skip_late,
    targets,
    negative_rows,
    recording_ids,
):
    signal = values[0].astype(jnp.float32)
    inner_gate = gates_first[0].astype(jnp.float32)
    outer_gate = gates_second[0].astype(jnp.float32)
    frames = signal.shape[-1]
    early_skip = skip_early[:, None]
    late_skip = skip_late[:, None]
    target_full = targets[0].astype(jnp.float32)
    unit_target = (
        target_full / jnp.sqrt(jnp.sum(target_full * target_full, axis=-1, keepdims=True) + EPSILON)
    ).astype(jnp.bfloat16)
    signal_spec, early_spec = split_pair(signal, filter_early)
    mixed_one = inverse(multiply(signal_spec, early_spec), frames)[0] + early_skip * signal
    hidden = inner_gate * mixed_one
    hidden_spec, late_spec = split_pair(hidden, filter_late)
    mixed_two = inverse(multiply(hidden_spec, late_spec), frames)[0] + late_skip * hidden
    output = outer_gate * mixed_two
    arrived = lax.all_to_all(
        output[None].astype(jnp.bfloat16), "seq", split_axis=2, concat_axis=1, tiled=True
    ).astype(jnp.float32)
    output_rows = jnp.transpose(arrived[0])
    radius = jnp.sqrt(jnp.sum(output_rows * output_rows, axis=-1, keepdims=True) + EPSILON)
    unit_rows = output_rows / radius
    anchors = unit_rows.astype(jnp.bfloat16)
    own_record = lax.axis_index("dp")
    record_count = recording_ids.shape[0]
    record_range = jnp.arange(record_count, dtype=jnp.int32)
    self_label = jnp.sum(jnp.where(record_range == own_record, recording_ids, 0))
    segment = anchors.shape[0]
    block_rows = negative_rows[0]
    block_count = block_rows.shape[0]
    block_size = segment // block_count
    column_ids = jnp.arange(segment, dtype=jnp.int32)
    initial = (
        jnp.zeros((segment,), jnp.float32),
        jnp.zeros((segment, anchors.shape[1]), jnp.float32),
    )
    shard_rows = lax.all_gather(unit_target[None], "dp", axis=0, tiled=True)

    def one_record(partial_value, member):
        pool_rows, record = member
        label = jnp.sum(jnp.where(record_range == record, recording_ids, 0))
        allowed = (label != self_label).astype(jnp.float32)
        matches = (block_rows[:, :, None] == (record * segment + column_ids)[None, None, :]).astype(
            jnp.float32
        )
        counts = jnp.sum(matches, axis=1) * allowed
        counts = jnp.broadcast_to(counts[:, None, :], (block_count, block_size, segment)).reshape(
            segment, segment
        )
        scores = (
            lax.dot_general(
                anchors, pool_rows, (((1,), (1,)), ((), ())), preferred_element_type=jnp.float32
            )
            * INVERSE_TEMP
        )
        weights = counts * jnp.exp(scores)
        numerator = jnp.dot(
            weights.astype(jnp.bfloat16), pool_rows, preferred_element_type=jnp.float32
        )
        return ((partial_value[0] + jnp.sum(weights, axis=-1), partial_value[1] + numerator), None)

    records = jnp.arange(shard_rows.shape[0], dtype=jnp.int32)
    summed = lax.scan(one_record, initial, (shard_rows, records))[0]
    unit_self = unit_target.astype(jnp.float32)
    positive = jnp.exp(jnp.sum(anchors.astype(jnp.float32) * unit_self, axis=-1) * INVERSE_TEMP)
    totals = positive + summed[0]
    anchor_grad = ((positive / totals - 1.0)[:, None] * unit_self + summed[1] / totals[:, None]) * (
        INVERSE_TEMP * LOSS_SCALE
    )
    frame_grad = (
        anchor_grad - unit_rows * jnp.sum(unit_rows * anchor_grad, axis=-1, keepdims=True)
    ) / radius
    arrived_back = lax.all_to_all(
        shortened(jnp.transpose(frame_grad)[None]), "seq", split_axis=1, concat_axis=2, tiled=True
    )
    cotangent = arrived_back[0]
    second_grad = (cotangent * mixed_two).astype(jnp.bfloat16)
    late_drive = cotangent * outer_gate
    back_late = spectrum(late_drive)
    late_pair = combine(
        multiply(back_late, conjugate(late_spec)), multiply(back_late, conjugate(hidden_spec))
    )
    hidden_back, late_update = inverse(late_pair, frames)
    hidden_grad = hidden_back + late_skip * late_drive
    first_grad = (hidden_grad * mixed_one).astype(jnp.bfloat16)
    early_drive = hidden_grad * inner_gate
    back_early = spectrum(early_drive)
    early_pair = combine(
        multiply(back_early, conjugate(early_spec)), multiply(back_early, conjugate(signal_spec))
    )
    signal_back, early_update = inverse(early_pair, frames)
    values_grad = (signal_back + early_skip * early_drive).astype(jnp.bfloat16)
    filter_sums = (
        lax.psum(early_update.astype(jnp.bfloat16), "dp").astype(jnp.float32),
        lax.psum(late_update.astype(jnp.bfloat16), "dp").astype(jnp.float32),
    )
    return (
        values_grad[None],
        first_grad[None],
        second_grad[None],
        filter_sums[0] / frames,
        filter_sums[1] / frames,
    )


def tables(frames):
    odd = 2 * np.arange(frames, dtype=np.int64) + 1
    period = 8 * frames
    circle = 2.0 * np.pi / period * np.arange(period)
    product = odd[:, None] * odd[None, :] % period
    highs, lows = [], []
    for wave in (np.cos(circle), np.sin(circle)):
        wave = wave.astype(np.float32)
        high = wave.astype(BF16)
        low = (wave - high.astype(np.float32)).astype(BF16)
        highs.append(high[product])
        lows.append(low[product])
    half = np.pi * odd / (4.0 * frames)
    turn = np.stack([np.cos(half), np.sin(half)]) / frames
    return np.stack(highs), np.stack(lows), turn.astype(np.float32)


def halves(value):
    high = value.astype(BF16)
    return high, (value - high.astype(F32)).astype(BF16)


def product(parts, table_high, table_low):
    high, low = parts
    total = jnp.dot(high, table_high, preferred_element_type=F32)
    if table_low is not None:
        total += jnp.dot(high, table_low, preferred_element_type=F32)
    if low is not None:
        total += jnp.dot(low, table_high, preferred_element_type=F32)
    return total


def kernel(
    sizes,
    values_ref, first_ref, second_ref, early_ref, late_ref, early_skip_ref, late_skip_ref,
    targets_ref, rows_ref, ids_ref, high_ref, low_ref, turn_ref,
    values_out, first_out, second_out, early_out, late_out,
    pool, out_send, out_recv, back_send, back_recv, reduce_send, reduce_recv,
    mixed_one, mixed_two, early_spec, late_spec, signal_spec, hidden_spec,
    pool_send_sem, pool_recv_sem, pass_send_sem, pass_recv_sem,
    out_send_sem, out_recv_sem, back_send_sem, back_recv_sem,
    reduce_send_sem, reduce_recv_sem, share_send_sem, share_recv_sem,
):
    records, stages = sizes
    chips = records // 2
    me = lax.axis_index("dp")
    here = lax.axis_index("seq")
    chip, core = me // 2, me % 2
    partner = chip * 2 + (1 - core)
    channels, frames = mixed_one.shape
    segment = pool.shape[1]
    depth = pool.shape[2]

    barrier = pltpu.get_barrier_semaphore()
    for k in range(1, records):
        pl.semaphore_signal(
            barrier, inc=1, device_id=(lax.rem(me + k, records), here), device_id_type=MESH
        )
    for k in range(1, stages):
        pl.semaphore_signal(
            barrier, inc=1, device_id=(me, lax.rem(here + k, stages)), device_id_type=MESH
        )

    def remote(source, target, send, recv, device):
        return pltpu.make_async_remote_copy(
            src_ref=source, dst_ref=target, send_sem=send, recv_sem=recv,
            device_id=device, device_id_type=MESH,
        )

    full = targets_ref[0].astype(F32)
    norm = jnp.sqrt(jnp.sum(full * full, axis=-1, keepdims=True) + EPSILON)
    pool[me] = (full / norm).astype(BF16)
    pl.semaphore_wait(barrier, records + stages - 2)

    def pool_copy(k):
        peer = lax.rem(chip + k, chips) * 2 + core
        return remote(pool.at[me], pool.at[me], pool_send_sem.at[k], pool_recv_sem.at[k], (peer, here))

    def pool_arrival(k):
        slot = lax.rem(chip + chips - k, chips) * 2 + core
        return slot, remote(
            pool.at[slot], pool.at[slot], pool_send_sem.at[k], pool_recv_sem.at[k], (slot, here)
        )

    def pass_copy(k):
        slot = lax.rem(chip + chips - k, chips) * 2 + core
        return remote(
            pool.at[slot], pool.at[slot], pass_send_sem.at[k], pass_recv_sem.at[k], (partner, here)
        )

    def pass_arrival(k):
        slot = lax.rem(chip + chips - k, chips) * 2 + (1 - core)
        return remote(
            pool.at[slot], pool.at[slot], pass_send_sem.at[k], pass_recv_sem.at[k], (partner, here)
        )

    for k in range(1, chips):
        pool_copy(k).start()
    pass_copy(0).start()

    def forward(parts):
        return tuple(product(parts, high_ref[i], low_ref[i]) for i in (0, 1))

    def inverse(cosine, sine, fine=True):
        total = None
        for i, wave in enumerate((cosine, sine)):
            part = product((wave.astype(BF16), None), high_ref[i], low_ref[i] if fine else None)
            total = part if total is None else total + part
        return total

    def unshifted(spec):
        cosine, sine = spec
        turn_cosine = turn_ref[0:1, :]
        turn_sine = turn_ref[1:2, :]
        return (
            cosine * turn_cosine + sine * turn_sine,
            sine * turn_cosine - cosine * turn_sine,
        )

    def keep(ref, spec):
        ref[0] = spec[0]
        ref[1] = spec[1]

    def convolved(spec, ref):
        cosine, sine = spec
        return inverse(cosine * ref[0] - sine * ref[1], cosine * ref[1] + sine * ref[0])

    def correlated(spec, ref, fine=True):
        cosine, sine = spec
        return inverse(cosine * ref[0] + sine * ref[1], sine * ref[0] - cosine * ref[1], fine)

    def column(row):
        return jnp.broadcast_to(row, (8, channels)).T[:, 0:1]

    early_skip = column(early_skip_ref[...])
    late_skip = column(late_skip_ref[...])

    keep(early_spec, unshifted(forward(halves(early_ref[...]))))
    keep(late_spec, unshifted(forward(halves(late_ref[...]))))
    spec = forward((values_ref[0], None))
    mixed_one[...] = convolved(spec, early_spec) + early_skip * values_ref[0].astype(F32)
    signal_waves = spec
    hidden = first_ref[0].astype(F32) * mixed_one[...]
    spec = forward((hidden.astype(BF16), None))
    mixed_two[...] = convolved(spec, late_spec) + late_skip * hidden

    output = second_ref[0].astype(F32) * mixed_two[...]
    for s in range(stages):
        out_send[s] = output[:, s * segment : (s + 1) * segment].astype(BF16)

    def exchange(k, send, recv, send_sem, recv_sem):
        peer = lax.rem(here + k, stages)
        return remote(send.at[peer], recv.at[here], send_sem.at[k], recv_sem.at[k], (me, peer))

    def exchange_arrival(k, send, recv, send_sem, recv_sem):
        peer = lax.rem(here + stages - k, stages)
        return remote(send.at[peer], recv.at[peer], send_sem.at[k], recv_sem.at[k], (me, peer))

    out_group = (out_send, out_recv, out_send_sem, out_recv_sem)
    back_group = (back_send, back_recv, back_send_sem, back_recv_sem)
    for k in range(1, stages):
        exchange(k, *out_group).start()
    out_recv[here] = out_send[here]
    keep(signal_spec, unshifted(signal_waves))
    keep(hidden_spec, unshifted(spec))

    for k in range(1, chips):
        pool_arrival(k)[1].wait_recv()
        pass_copy(k).start()

    blocks = rows_ref.shape[1]
    draws = rows_ref.shape[2]
    block_size = segment // blocks
    frame_block = lax.broadcasted_iota(jnp.int32, (draws, segment), 1) // block_size
    counts = jnp.zeros((records * segment, segment), F32)
    position = lax.broadcasted_iota(jnp.int32, (records * segment, draws), 0)
    for b in range(blocks):
        matches = jnp.where(position == rows_ref[0, b : b + 1, :], 1.0, 0.0).astype(BF16)
        chosen = jnp.where(frame_block == b, 1.0, 0.0).astype(BF16)
        counts += jnp.dot(matches, chosen, preferred_element_type=F32)

    self_units = pool[me].astype(F32).T

    for k in range(1, stages):
        exchange_arrival(k, *out_group).wait_recv()
    rows = jnp.concatenate([out_recv[s] for s in range(stages)], axis=0).astype(F32)
    radius = jnp.sqrt(jnp.sum(rows * rows, axis=0, keepdims=True) + EPSILON)
    unit_rows = rows / radius
    anchors = unit_rows.astype(BF16)
    positive = jnp.exp(jnp.sum(anchors.astype(F32) * self_units, axis=0, keepdims=True) * INVERSE_TEMP)

    for k in range(chips):
        pass_arrival(k).wait_recv()

    totals = positive
    numerator = jnp.zeros((segment, depth), F32)
    for q in range(records):
        units = pool[q]
        allowed = jnp.where(ids_ref[q] != ids_ref[me], 1.0, 0.0).astype(F32)
        scores = jnp.dot(units, anchors, preferred_element_type=F32) * INVERSE_TEMP
        weights = counts[q * segment : (q + 1) * segment, :] * allowed * jnp.exp(scores)
        totals += jnp.sum(weights, axis=0, keepdims=True)
        numerator += jnp.dot(weights.T.astype(BF16), units, preferred_element_type=F32)
    anchor_grad = ((positive / totals - 1.0) * self_units + numerator.T / totals) * (
        INVERSE_TEMP * LOSS_SCALE
    )
    frame_grad = (
        anchor_grad - unit_rows * jnp.sum(unit_rows * anchor_grad, axis=0, keepdims=True)
    ) / radius
    for s in range(stages):
        back_send[s] = frame_grad[s * channels : (s + 1) * channels, :].astype(BF16)
    for k in range(1, stages):
        exchange(k, *back_group).start()
    back_recv[here] = back_send[here]
    for k in range(1, stages):
        exchange_arrival(k, *back_group).wait_recv()

    cotangent = jnp.concatenate([back_recv[s] for s in range(stages)], axis=1).astype(F32)
    second_out[0] = (cotangent * mixed_two[...]).astype(BF16)
    late_drive = cotangent * second_ref[0].astype(F32)
    spec = forward((late_drive.astype(BF16), None))

    shard = channels // records

    def spread(which, update):
        for r in range(records):
            reduce_send[which, r] = update[r * shard : (r + 1) * shard, :].astype(BF16)
        for k in range(1, records):
            peer = lax.rem(me + k, records)
            remote(
                reduce_send.at[which, peer], reduce_recv.at[which, me],
                reduce_send_sem.at[which, k], reduce_recv_sem.at[which, k], (peer, here),
            ).start()

    def share(which, target):
        for k in range(1, records):
            peer = lax.rem(me + records - k, records)
            remote(
                reduce_send.at[which, peer], reduce_recv.at[which, peer],
                reduce_send_sem.at[which, k], reduce_recv_sem.at[which, k], (peer, here),
            ).wait_recv()
        total = reduce_send[which, me].astype(F32)
        for k in range(1, records):
            total += reduce_recv[which, lax.rem(me + records - k, records)].astype(F32)
        target[me] = total.astype(BF16)
        for k in range(1, records):
            peer = lax.rem(me + k, records)
            remote(
                target.at[me], target.at[me],
                share_send_sem.at[which, k], share_recv_sem.at[which, k], (peer, here),
            ).start()

    spread(1, correlated(spec, hidden_spec, fine=False))
    hidden_grad = correlated(spec, late_spec) + late_skip * late_drive
    first_out[0] = (hidden_grad * mixed_one[...]).astype(BF16)
    early_drive = hidden_grad * first_ref[0].astype(F32)
    spec = forward((early_drive.astype(BF16), None))
    share(1, late_out)
    spread(0, correlated(spec, signal_spec, fine=False))
    values_out[0] = (correlated(spec, early_spec) + early_skip * early_drive).astype(BF16)
    share(0, early_out)

    for k in range(1, chips):
        pool_copy(k).wait_send()
    for k in range(chips):
        pass_copy(k).wait_send()
    for k in range(1, stages):
        exchange(k, *out_group).wait_send()
        exchange(k, *back_group).wait_send()
    for which, target in ((1, late_out), (0, early_out)):
        for k in range(1, records):
            peer = lax.rem(me + k, records)
            remote(
                reduce_send.at[which, peer], reduce_recv.at[which, me],
                reduce_send_sem.at[which, k], reduce_recv_sem.at[which, k], (peer, here),
            ).wait_send()
            source = lax.rem(me + records - k, records)
            shared = remote(
                target.at[source], target.at[source],
                share_send_sem.at[which, k], share_recv_sem.at[which, k], (source, here),
            )
            shared.wait_recv()
            shared.wait_send()


def finish(frames, *refs):
    for source, target in zip(refs[:3], refs[5:8]):
        target[...] = source[...]
    for source, target in zip(refs[3:5], refs[8:]):
        target[...] = source[...].astype(F32) / frames


def local(
    records, stages,
    values, gates_first, gates_second, filter_early, filter_late, skip_early, skip_late,
    targets, negative_rows, recording_ids,
):
    _, channels, frames = values.shape
    _, segment, depth = targets.shape
    if 8 * frames * frames > TABLE_BYTES:
        return local_large(
            values, gates_first, gates_second, filter_early, filter_late, skip_early, skip_late,
            targets, negative_rows, recording_ids,
        )
    high, low, turn = tables(frames)
    shard = channels // records
    vmem = pl.BlockSpec(memory_space=pltpu.VMEM)
    stream = jax.ShapeDtypeStruct(values.shape, BF16)
    update = jax.ShapeDtypeStruct((records, shard, frames), BF16)
    exchange = pltpu.VMEM((stages, channels, segment), BF16)
    reduce = pltpu.VMEM((2, records, shard, frames), BF16)
    plane = pltpu.VMEM((channels, frames), F32)
    spec = pltpu.VMEM((2, channels, frames), F32)
    semaphores = pltpu.SemaphoreType.DMA
    chips = records // 2
    results = pl.pallas_call(
        functools.partial(kernel, (records, stages)),
        out_shape=(stream, stream, stream, update, update),
        in_specs=[vmem] * 9 + [pl.BlockSpec(memory_space=pltpu.SMEM)] + [vmem] * 3,
        out_specs=(vmem,) * 5,
        scratch_shapes=[
            pltpu.VMEM((records, segment, depth), BF16),
            exchange, exchange, exchange, exchange, reduce, reduce,
            plane, plane, spec, spec, spec, spec,
            semaphores((chips,)), semaphores((chips,)), semaphores((chips,)), semaphores((chips,)),
            semaphores((stages,)), semaphores((stages,)), semaphores((stages,)), semaphores((stages,)),
            semaphores((2, records)), semaphores((2, records)),
            semaphores((2, records)), semaphores((2, records)),
        ],
        compiler_params=pltpu.CompilerParams(
            collective_id=0, has_side_effects=True, vmem_limit_bytes=63 * 1024 * 1024
        ),
    )(
        values, gates_first, gates_second, filter_early, filter_late,
        skip_early[None], skip_late[None], targets, negative_rows, recording_ids,
        jnp.asarray(high), jnp.asarray(low), jnp.asarray(turn),
    )
    wide = jax.ShapeDtypeStruct(update.shape, F32)
    *streams, early, late = pl.pallas_call(
        functools.partial(finish, frames),
        out_shape=(stream, stream, stream, wide, wide),
        in_specs=[vmem] * 5,
        out_specs=(vmem,) * 5,
        compiler_params=pltpu.CompilerParams(vmem_limit_bytes=63 * 1024 * 1024),
    )(*results)
    return (*streams, early.reshape(channels, frames), late.reshape(channels, frames))


def solution(mesh):
    placed = (
        P("dp", "seq", None),
        P("dp", "seq", None),
        P("dp", "seq", None),
        P("seq", None),
        P("seq", None),
        P("seq"),
        P("seq"),
        P("dp", "seq", None),
        P("dp", "seq", None),
        P(),
    )
    return jax.shard_map(
        functools.partial(local, mesh.shape["dp"], mesh.shape["seq"]),
        mesh=mesh,
        in_specs=placed,
        out_specs=(
            P("dp", "seq", None),
            P("dp", "seq", None),
            P("dp", "seq", None),
            P("seq", None),
            P("seq", None),
        ),
        check_vma=False,
    )
```

```python
import functools
import math

import jax
import jax.numpy as jnp
import numpy as np
from jax import lax
from jax.experimental import pallas as pl
from jax.experimental.pallas import tpu as pltpu
from jax.sharding import PartitionSpec as P

EPSILON = 1e-06
INVERSE_TEMP = 10.0
LOSS_SCALE = 256.0
MESH = pl.DeviceIdType.MESH
F32 = jnp.float32
BF16 = jnp.bfloat16
TABLE_BYTES = 16 * 1024 * 1024
INNER_WIDTH = 128
HIGHEST = lax.Precision.HIGHEST


def shortened(value):

    def short(part):
        return part.astype(jnp.bfloat16) if part.dtype == jnp.float32 else part

    return jax.tree.map(short, value)


def twiddle(row_count, column_count, length, direction):
    product = (
        jnp.arange(row_count, dtype=jnp.int32)[:, None]
        * jnp.arange(column_count, dtype=jnp.int32)[None, :]
        % length
    )
    angles = direction * 2.0 * math.pi / length * product.astype(jnp.float32)
    return (jnp.cos(angles), jnp.sin(angles))


def complex_table(cosines, sines, with_imaginary):
    upper = jnp.concatenate([cosines, sines], axis=1)
    if not with_imaginary:
        return upper
    lower = jnp.concatenate([-sines, cosines], axis=1)
    return jnp.concatenate([upper, lower], axis=0)


def transform(real_part, imaginary, direction, length):
    used = real_part.shape[-1]
    with_imaginary = imaginary is not None
    outer_size = length // INNER_WIDTH
    used_rows = used // INNER_WIDTH
    lead = real_part.shape[:-1]
    folded_real = real_part.reshape(lead + (used_rows, INNER_WIDTH))
    cosines, sines = twiddle(used_rows, outer_size, outer_size, direction)
    table = complex_table(cosines, sines, with_imaginary)
    if with_imaginary:
        stacked = jnp.concatenate(
            [folded_real, imaginary.reshape(lead + (used_rows, INNER_WIDTH))], axis=-2
        )
    else:
        stacked = folded_real
    section = jnp.einsum("...ab,ak->...kb", stacked, table, precision=HIGHEST)
    section_real = section[..., :outer_size, :]
    section_imaginary = section[..., outer_size:, :]
    turn_cosine, turn_sine = twiddle(outer_size, INNER_WIDTH, length, direction)
    turned_real = section_real * turn_cosine - section_imaginary * turn_sine
    turned_imaginary = section_real * turn_sine + section_imaginary * turn_cosine
    inner_cosine, inner_sine = twiddle(INNER_WIDTH, INNER_WIDTH, INNER_WIDTH, direction)
    inner_table = complex_table(inner_cosine, inner_sine, True)
    second = jnp.einsum(
        "...ab,bk->...ak",
        jnp.concatenate([turned_real, turned_imaginary], axis=-1),
        inner_table,
        precision=HIGHEST,
    )
    final_real = jnp.swapaxes(second[..., :INNER_WIDTH], -1, -2).reshape(lead + (length,))
    final_imaginary = jnp.swapaxes(second[..., INNER_WIDTH:], -1, -2).reshape(lead + (length,))
    return (final_real, final_imaginary)


def spectrum(signal):
    return transform(signal, None, -1.0, 2 * signal.shape[-1])


def split_pair(first_signal, second_signal):
    spec_real, spec_imaginary = transform(
        first_signal, second_signal, -1.0, 2 * first_signal.shape[-1]
    )
    mirror_real = jnp.roll(jnp.flip(spec_real, -1), 1, -1)
    mirror_imaginary = jnp.roll(jnp.flip(spec_imaginary, -1), 1, -1)
    first_spec = ((spec_real + mirror_real) * 0.5, (spec_imaginary - mirror_imaginary) * 0.5)
    second_spec = ((spec_imaginary + mirror_imaginary) * 0.5, (mirror_real - spec_real) * 0.5)
    return (first_spec, second_spec)


def multiply(left_side, right_side):
    return (
        left_side[0] * right_side[0] - left_side[1] * right_side[1],
        left_side[0] * right_side[1] + left_side[1] * right_side[0],
    )


def conjugate(spec):
    return (spec[0], -spec[1])


def combine(left_side, right_side):
    return (left_side[0] - right_side[1], left_side[1] + right_side[0])


def inverse(spec, frames):
    length = spec[0].shape[-1]
    out_real, out_imaginary = transform(spec[0], spec[1], 1.0, length)
    factor = 1.0 / length
    return (out_real[..., :frames] * factor, out_imaginary[..., :frames] * factor)


def local_large(
    values,
    gates_first,
    gates_second,
    filter_early,
    filter_late,
    skip_early,
    skip_late,
    targets,
    negative_rows,
    recording_ids,
):
    signal = values[0].astype(jnp.float32)
    inner_gate = gates_first[0].astype(jnp.float32)
    outer_gate = gates_second[0].astype(jnp.float32)
    frames = signal.shape[-1]
    early_skip = skip_early[:, None]
    late_skip = skip_late[:, None]
    target_full = targets[0].astype(jnp.float32)
    unit_target = (
        target_full / jnp.sqrt(jnp.sum(target_full * target_full, axis=-1, keepdims=True) + EPSILON)
    ).astype(jnp.bfloat16)
    signal_spec, early_spec = split_pair(signal, filter_early)
    mixed_one = inverse(multiply(signal_spec, early_spec), frames)[0] + early_skip * signal
    hidden = inner_gate * mixed_one
    hidden_spec, late_spec = split_pair(hidden, filter_late)
    mixed_two = inverse(multiply(hidden_spec, late_spec), frames)[0] + late_skip * hidden
    output = outer_gate * mixed_two
    arrived = lax.all_to_all(
        output[None].astype(jnp.bfloat16), "seq", split_axis=2, concat_axis=1, tiled=True
    ).astype(jnp.float32)
    output_rows = jnp.transpose(arrived[0])
    radius = jnp.sqrt(jnp.sum(output_rows * output_rows, axis=-1, keepdims=True) + EPSILON)
    unit_rows = output_rows / radius
    anchors = unit_rows.astype(jnp.bfloat16)
    own_record = lax.axis_index("dp")
    record_count = recording_ids.shape[0]
    record_range = jnp.arange(record_count, dtype=jnp.int32)
    self_label = jnp.sum(jnp.where(record_range == own_record, recording_ids, 0))
    segment = anchors.shape[0]
    block_rows = negative_rows[0]
    block_count = block_rows.shape[0]
    block_size = segment // block_count
    column_ids = jnp.arange(segment, dtype=jnp.int32)
    initial = (
        jnp.zeros((segment,), jnp.float32),
        jnp.zeros((segment, anchors.shape[1]), jnp.float32),
    )
    shard_rows = lax.all_gather(unit_target[None], "dp", axis=0, tiled=True)

    def one_record(partial_value, member):
        pool_rows, record = member
        label = jnp.sum(jnp.where(record_range == record, recording_ids, 0))
        allowed = (label != self_label).astype(jnp.float32)
        matches = (block_rows[:, :, None] == (record * segment + column_ids)[None, None, :]).astype(
            jnp.float32
        )
        counts = jnp.sum(matches, axis=1) * allowed
        counts = jnp.broadcast_to(counts[:, None, :], (block_count, block_size, segment)).reshape(
            segment, segment
        )
        scores = (
            lax.dot_general(
                anchors, pool_rows, (((1,), (1,)), ((), ())), preferred_element_type=jnp.float32
            )
            * INVERSE_TEMP
        )
        weights = counts * jnp.exp(scores)
        numerator = jnp.dot(
            weights.astype(jnp.bfloat16), pool_rows, preferred_element_type=jnp.float32
        )
        return ((partial_value[0] + jnp.sum(weights, axis=-1), partial_value[1] + numerator), None)

    records = jnp.arange(shard_rows.shape[0], dtype=jnp.int32)
    summed = lax.scan(one_record, initial, (shard_rows, records))[0]
    unit_self = unit_target.astype(jnp.float32)
    positive = jnp.exp(jnp.sum(anchors.astype(jnp.float32) * unit_self, axis=-1) * INVERSE_TEMP)
    totals = positive + summed[0]
    anchor_grad = ((positive / totals - 1.0)[:, None] * unit_self + summed[1] / totals[:, None]) * (
        INVERSE_TEMP * LOSS_SCALE
    )
    frame_grad = (
        anchor_grad - unit_rows * jnp.sum(unit_rows * anchor_grad, axis=-1, keepdims=True)
    ) / radius
    arrived_back = lax.all_to_all(
        shortened(jnp.transpose(frame_grad)[None]), "seq", split_axis=1, concat_axis=2, tiled=True
    )
    cotangent = arrived_back[0]
    second_grad = (cotangent * mixed_two).astype(jnp.bfloat16)
    late_drive = cotangent * outer_gate
    back_late = spectrum(late_drive)
    late_pair = combine(
        multiply(back_late, conjugate(late_spec)), multiply(back_late, conjugate(hidden_spec))
    )
    hidden_back, late_update = inverse(late_pair, frames)
    hidden_grad = hidden_back + late_skip * late_drive
    first_grad = (hidden_grad * mixed_one).astype(jnp.bfloat16)
    early_drive = hidden_grad * inner_gate
    back_early = spectrum(early_drive)
    early_pair = combine(
        multiply(back_early, conjugate(early_spec)), multiply(back_early, conjugate(signal_spec))
    )
    signal_back, early_update = inverse(early_pair, frames)
    values_grad = (signal_back + early_skip * early_drive).astype(jnp.bfloat16)
    filter_sums = (
        lax.psum(early_update.astype(jnp.bfloat16), "dp").astype(jnp.float32),
        lax.psum(late_update.astype(jnp.bfloat16), "dp").astype(jnp.float32),
    )
    return (
        values_grad[None],
        first_grad[None],
        second_grad[None],
        filter_sums[0] / frames,
        filter_sums[1] / frames,
    )


def tables(frames):
    odd = 2 * np.arange(frames, dtype=np.int64) + 1
    period = 8 * frames
    circle = 2.0 * np.pi / period * np.arange(period)
    product = odd[:, None] * odd[None, :] % period
    highs, lows = [], []
    for wave in (np.cos(circle), np.sin(circle)):
        wave = wave.astype(np.float32)
        high = wave.astype(BF16)
        low = (wave - high.astype(np.float32)).astype(BF16)
        highs.append(high[product])
        lows.append(low[product])
    half = np.pi * odd / (4.0 * frames)
    turn = np.stack([np.cos(half), np.sin(half)]) / frames
    return np.stack(highs), np.stack(lows), turn.astype(np.float32)


def halves(value):
    high = value.astype(BF16)
    return high, (value - high.astype(F32)).astype(BF16)


def product(parts, table_high, table_low):
    high, low = parts
    total = jnp.dot(high, table_high, preferred_element_type=F32)
    if table_low is not None:
        total += jnp.dot(high, table_low, preferred_element_type=F32)
    if low is not None:
        total += jnp.dot(low, table_high, preferred_element_type=F32)
    return total


def kernel(
    sizes,
    values_ref, first_ref, second_ref, early_ref, late_ref, early_skip_ref, late_skip_ref,
    targets_ref, rows_ref, ids_ref, high_ref, low_ref, turn_ref,
    values_out, first_out, second_out, early_out, late_out,
    pool, out_send, out_recv, back_send, back_recv, reduce_send, reduce_recv,
    mixed_one, mixed_two, early_spec, late_spec, signal_spec, hidden_spec,
    pool_send_sem, pool_recv_sem, pass_send_sem, pass_recv_sem,
    out_send_sem, out_recv_sem, back_send_sem, back_recv_sem,
    reduce_send_sem, reduce_recv_sem, share_send_sem, share_recv_sem,
):
    records, stages = sizes
    chips = records // 2
    me = lax.axis_index("dp")
    here = lax.axis_index("seq")
    chip, core = me // 2, me % 2
    partner = chip * 2 + (1 - core)
    channels, frames = mixed_one.shape
    segment = pool.shape[1]
    depth = pool.shape[2]

    barrier = pltpu.get_barrier_semaphore()
    for k in range(1, records):
        pl.semaphore_signal(
            barrier, inc=1, device_id=(lax.rem(me + k, records), here), device_id_type=MESH
        )
    for k in range(1, stages):
        pl.semaphore_signal(
            barrier, inc=1, device_id=(me, lax.rem(here + k, stages)), device_id_type=MESH
        )

    def remote(source, target, send, recv, device):
        return pltpu.make_async_remote_copy(
            src_ref=source, dst_ref=target, send_sem=send, recv_sem=recv,
            device_id=device, device_id_type=MESH,
        )

    full = targets_ref[0].astype(F32)
    norm = jnp.sqrt(jnp.sum(full * full, axis=-1, keepdims=True) + EPSILON)
    pool[me] = (full / norm).astype(BF16)
    pl.semaphore_wait(barrier, records + stages - 2)

    def pool_copy(k):
        peer = lax.rem(chip + k, chips) * 2 + core
        return remote(pool.at[me], pool.at[me], pool_send_sem.at[k], pool_recv_sem.at[k], (peer, here))

    def pool_arrival(k):
        slot = lax.rem(chip + chips - k, chips) * 2 + core
        return slot, remote(
            pool.at[slot], pool.at[slot], pool_send_sem.at[k], pool_recv_sem.at[k], (slot, here)
        )

    def pass_copy(k):
        slot = lax.rem(chip + chips - k, chips) * 2 + core
        return remote(
            pool.at[slot], pool.at[slot], pass_send_sem.at[k], pass_recv_sem.at[k], (partner, here)
        )

    def pass_arrival(k):
        slot = lax.rem(chip + chips - k, chips) * 2 + (1 - core)
        return remote(
            pool.at[slot], pool.at[slot], pass_send_sem.at[k], pass_recv_sem.at[k], (partner, here)
        )

    for k in range(1, chips):
        pool_copy(k).start()
    pass_copy(0).start()

    def forward(parts):
        return tuple(product(parts, high_ref[i], low_ref[i]) for i in (0, 1))

    def inverse(cosine, sine, fine=True):
        total = None
        for i, wave in enumerate((cosine, sine)):
            part = product((wave.astype(BF16), None), high_ref[i], low_ref[i] if fine else None)
            total = part if total is None else total + part
        return total

    def unshifted(spec):
        cosine, sine = spec
        turn_cosine = turn_ref[0:1, :]
        turn_sine = turn_ref[1:2, :]
        return (
            cosine * turn_cosine + sine * turn_sine,
            sine * turn_cosine - cosine * turn_sine,
        )

    def keep(ref, spec, part=slice(None)):
        ref[0, part, :] = spec[0]
        ref[1, part, :] = spec[1]

    def convolved(spec, ref, part):
        cosine, sine = spec
        other_cosine, other_sine = ref[0, part, :], ref[1, part, :]
        return inverse(
            cosine * other_cosine - sine * other_sine, cosine * other_sine + sine * other_cosine
        )

    def correlated(spec, ref, fine=True):
        cosine, sine = spec
        return inverse(cosine * ref[0] + sine * ref[1], sine * ref[0] - cosine * ref[1], fine)

    def column(row):
        return jnp.broadcast_to(row, (8, channels)).T[:, 0:1]

    early_skip = column(early_skip_ref[...])
    late_skip = column(late_skip_ref[...])

    keep(early_spec, unshifted(forward(halves(early_ref[...]))))
    keep(late_spec, unshifted(forward(halves(late_ref[...]))))
    def exchange(k, send, recv, send_sem, recv_sem, part):
        peer = lax.rem(here + k, stages)
        return remote(
            send.at[peer, part], recv.at[here, part], send_sem.at[k], recv_sem.at[k], (me, peer)
        )

    def exchange_arrival(k, send, recv, send_sem, recv_sem, part):
        peer = lax.rem(here + stages - k, stages)
        return remote(
            send.at[peer, part], recv.at[peer, part], send_sem.at[k], recv_sem.at[k], (me, peer)
        )

    width = channels // out_send_sem.shape[0]
    out_groups = [
        (out_send, out_recv, out_send_sem.at[h], out_recv_sem.at[h], pl.ds(h * width, width))
        for h in range(out_send_sem.shape[0])
    ]
    back_group = (back_send, back_recv, back_send_sem, back_recv_sem, pl.ds(0, channels))
    kept = []
    for h, group in enumerate(out_groups):
        part = slice(h * width, (h + 1) * width)
        signal = values_ref[0, part, :]
        signal_waves = forward((signal, None))
        mixed = convolved(signal_waves, early_spec, part) + early_skip[part] * signal.astype(F32)
        mixed_one[part, :] = mixed
        hidden = first_ref[0, part, :].astype(F32) * mixed
        hidden_waves = forward((hidden.astype(BF16), None))
        mixed = convolved(hidden_waves, late_spec, part) + late_skip[part] * hidden
        mixed_two[part, :] = mixed
        output = (second_ref[0, part, :].astype(F32) * mixed).astype(BF16)
        for s in range(stages):
            out_send[s, part, :] = output[:, s * segment : (s + 1) * segment]
        for k in range(1, stages):
            exchange(k, *group).start()
        kept.append((part, signal_waves, hidden_waves))
    out_recv[here] = out_send[here]
    for part, signal_waves, hidden_waves in kept:
        keep(signal_spec, unshifted(signal_waves), part)
        keep(hidden_spec, unshifted(hidden_waves), part)

    for k in range(1, chips):
        pool_arrival(k)[1].wait_recv()
        pass_copy(k).start()

    blocks = rows_ref.shape[1]
    draws = rows_ref.shape[2]
    block_size = segment // blocks
    frame_block = lax.broadcasted_iota(jnp.int32, (draws, segment), 1) // block_size
    counts = jnp.zeros((records * segment, segment), F32)
    position = lax.broadcasted_iota(jnp.int32, (records * segment, draws), 0)
    for b in range(blocks):
        matches = jnp.where(position == rows_ref[0, b : b + 1, :], 1.0, 0.0).astype(BF16)
        chosen = jnp.where(frame_block == b, 1.0, 0.0).astype(BF16)
        counts += jnp.dot(matches, chosen, preferred_element_type=F32)

    self_units = pool[me].astype(F32).T

    for group in out_groups:
        for k in range(1, stages):
            exchange_arrival(k, *group).wait_recv()
    rows = jnp.concatenate([out_recv[s] for s in range(stages)], axis=0).astype(F32)
    radius = jnp.sqrt(jnp.sum(rows * rows, axis=0, keepdims=True) + EPSILON)
    unit_rows = rows / radius
    anchors = unit_rows.astype(BF16)
    positive = jnp.exp(jnp.sum(anchors.astype(F32) * self_units, axis=0, keepdims=True) * INVERSE_TEMP)

    for k in range(chips):
        pass_arrival(k).wait_recv()

    totals = positive
    numerator = jnp.zeros((segment, depth), F32)
    for q in range(records):
        units = pool[q]
        allowed = jnp.where(ids_ref[q] != ids_ref[me], 1.0, 0.0).astype(F32)
        scores = jnp.dot(units, anchors, preferred_element_type=F32) * INVERSE_TEMP
        weights = counts[q * segment : (q + 1) * segment, :] * allowed * jnp.exp(scores)
        totals += jnp.sum(weights, axis=0, keepdims=True)
        numerator += jnp.dot(weights.T.astype(BF16), units, preferred_element_type=F32)
    anchor_grad = ((positive / totals - 1.0) * self_units + numerator.T / totals) * (
        INVERSE_TEMP * LOSS_SCALE
    )
    frame_grad = (
        anchor_grad - unit_rows * jnp.sum(unit_rows * anchor_grad, axis=0, keepdims=True)
    ) / radius
    for s in range(stages):
        back_send[s] = frame_grad[s * channels : (s + 1) * channels, :].astype(BF16)
    for k in range(1, stages):
        exchange(k, *back_group).start()
    back_recv[here] = back_send[here]
    for k in range(1, stages):
        exchange_arrival(k, *back_group).wait_recv()

    cotangent = jnp.concatenate([back_recv[s] for s in range(stages)], axis=1).astype(F32)
    second_out[0] = (cotangent * mixed_two[...]).astype(BF16)
    late_drive = cotangent * second_ref[0].astype(F32)
    spec = forward((late_drive.astype(BF16), None))

    shard = channels // records

    def spread(which, update):
        for r in range(records):
            reduce_send[which, r] = update[r * shard : (r + 1) * shard, :].astype(BF16)
        for k in range(1, records):
            peer = lax.rem(me + k, records)
            remote(
                reduce_send.at[which, peer], reduce_recv.at[which, me],
                reduce_send_sem.at[which, k], reduce_recv_sem.at[which, k], (peer, here),
            ).start()

    def share(which, target):
        for k in range(1, records):
            peer = lax.rem(me + records - k, records)
            remote(
                reduce_send.at[which, peer], reduce_recv.at[which, peer],
                reduce_send_sem.at[which, k], reduce_recv_sem.at[which, k], (peer, here),
            ).wait_recv()
        total = reduce_send[which, me].astype(F32)
        for k in range(1, records):
            total += reduce_recv[which, lax.rem(me + records - k, records)].astype(F32)
        target[me] = total.astype(BF16)
        for k in range(1, records):
            peer = lax.rem(me + k, records)
            remote(
                target.at[me], target.at[me],
                share_send_sem.at[which, k], share_recv_sem.at[which, k], (peer, here),
            ).start()

    spread(1, correlated(spec, hidden_spec, fine=False))
    hidden_grad = correlated(spec, late_spec) + late_skip * late_drive
    first_out[0] = (hidden_grad * mixed_one[...]).astype(BF16)
    early_drive = hidden_grad * first_ref[0].astype(F32)
    spec = forward((early_drive.astype(BF16), None))
    share(1, late_out)
    spread(0, correlated(spec, signal_spec, fine=False))
    values_out[0] = (correlated(spec, early_spec) + early_skip * early_drive).astype(BF16)
    share(0, early_out)

    for k in range(1, chips):
        pool_copy(k).wait_send()
    for k in range(chips):
        pass_copy(k).wait_send()
    for k in range(1, stages):
        for group in out_groups:
            exchange(k, *group).wait_send()
        exchange(k, *back_group).wait_send()
    for which, target in ((1, late_out), (0, early_out)):
        for k in range(1, records):
            peer = lax.rem(me + k, records)
            remote(
                reduce_send.at[which, peer], reduce_recv.at[which, me],
                reduce_send_sem.at[which, k], reduce_recv_sem.at[which, k], (peer, here),
            ).wait_send()
            source = lax.rem(me + records - k, records)
            shared = remote(
                target.at[source], target.at[source],
                share_send_sem.at[which, k], share_recv_sem.at[which, k], (source, here),
            )
            shared.wait_recv()
            shared.wait_send()


def finish(frames, *refs):
    for source, target in zip(refs[:3], refs[5:8]):
        target[...] = source[...]
    for source, target in zip(refs[3:5], refs[8:]):
        target[...] = source[...].astype(F32) / frames


def local(
    records, stages,
    values, gates_first, gates_second, filter_early, filter_late, skip_early, skip_late,
    targets, negative_rows, recording_ids,
):
    _, channels, frames = values.shape
    _, segment, depth = targets.shape
    if 8 * frames * frames > TABLE_BYTES:
        return local_large(
            values, gates_first, gates_second, filter_early, filter_late, skip_early, skip_late,
            targets, negative_rows, recording_ids,
        )
    high, low, turn = tables(frames)
    shard = channels // records
    vmem = pl.BlockSpec(memory_space=pltpu.VMEM)
    stream = jax.ShapeDtypeStruct(values.shape, BF16)
    update = jax.ShapeDtypeStruct((records, shard, frames), BF16)
    exchange = pltpu.VMEM((stages, channels, segment), BF16)
    reduce = pltpu.VMEM((2, records, shard, frames), BF16)
    plane = pltpu.VMEM((channels, frames), F32)
    spec = pltpu.VMEM((2, channels, frames), F32)
    semaphores = pltpu.SemaphoreType.DMA
    chips = records // 2
    shares = 2 if channels % 256 == 0 else 1
    results = pl.pallas_call(
        functools.partial(kernel, (records, stages)),
        out_shape=(stream, stream, stream, update, update),
        in_specs=[vmem] * 9 + [pl.BlockSpec(memory_space=pltpu.SMEM)] + [vmem] * 3,
        out_specs=(vmem,) * 5,
        scratch_shapes=[
            pltpu.VMEM((records, segment, depth), BF16),
            exchange, exchange, exchange, exchange, reduce, reduce,
            plane, plane, spec, spec, spec, spec,
            semaphores((chips,)), semaphores((chips,)), semaphores((chips,)), semaphores((chips,)),
            semaphores((shares, stages)), semaphores((shares, stages)),
            semaphores((stages,)), semaphores((stages,)),
            semaphores((2, records)), semaphores((2, records)),
            semaphores((2, records)), semaphores((2, records)),
        ],
        compiler_params=pltpu.CompilerParams(
            collective_id=0, has_side_effects=True, vmem_limit_bytes=63 * 1024 * 1024
        ),
    )(
        values, gates_first, gates_second, filter_early, filter_late,
        skip_early[None], skip_late[None], targets, negative_rows, recording_ids,
        jnp.asarray(high), jnp.asarray(low), jnp.asarray(turn),
    )
    wide = jax.ShapeDtypeStruct(update.shape, F32)
    *streams, early, late = pl.pallas_call(
        functools.partial(finish, frames),
        out_shape=(stream, stream, stream, wide, wide),
        in_specs=[vmem] * 5,
        out_specs=(vmem,) * 5,
        compiler_params=pltpu.CompilerParams(vmem_limit_bytes=63 * 1024 * 1024),
    )(*results)
    return (*streams, early.reshape(channels, frames), late.reshape(channels, frames))


def solution(mesh):
    placed = (
        P("dp", "seq", None),
        P("dp", "seq", None),
        P("dp", "seq", None),
        P("seq", None),
        P("seq", None),
        P("seq"),
        P("seq"),
        P("dp", "seq", None),
        P("dp", "seq", None),
        P(),
    )
    return jax.shard_map(
        functools.partial(local, mesh.shape["dp"], mesh.shape["seq"]),
        mesh=mesh,
        in_specs=placed,
        out_specs=(
            P("dp", "seq", None),
            P("dp", "seq", None),
            P("dp", "seq", None),
            P("seq", None),
            P("seq", None),
        ),
        check_vma=False,
    )
```
